256 devices in a mesh: cols: 128 (over x, y, z), rows: 2 (over core).
Axes of the slice: x: 4, y: 4, z: 8, core: 2. Of those that a mesh axis runs over, the one named last changes fastest.
Arguments:
- activations: bfloat16 [256, 65536], P('rows', 'cols'), may hold values from 0 to 16
- weights: bfloat16 [2, 512, 40, 128, 128], P(None, 'cols', 'rows'), may hold values from -0.15625 to 0.15625
- biases: float32 [2, 65536], P(None, 'cols'), may hold values from -6 to 2
- pattern: int32 [2, 512, 40], P(None, 'cols'), may hold values from 0 to 511, as said below
- counts: int32 [2, 512], P(None, 'cols'), may hold values from 1 to 40, 10240 in all within a row
Outputs:
- result: bfloat16 [256, 65536], P('rows', 'cols')
The draws below stay inside these ranges and needn't reach their ends.
Inputs may be any that keep to these rules, and one draw needn't show every extreme that they name: `pattern`: the 40 entries of a column block are distinct. All entries of the 4 column blocks held by one index of cols, live or not, name at most 1 different blocks among the 4 blocks held by any one index of cols, and exactly 1 for some. In each layer the counts sum to 10240.
All inputs are finite; a program needn't handle non-finite values. No bound on the sum of `counts` on one device may be relied on, other than what follows from the above.
Results may differ from the reference program's by a relative error of at most 0.0047.
Values may be sent and summed in bfloat16 or wider, within the bound.
A program may use at most 128 MiB of HBM per device.

```python
import math
import jax
import jax.numpy as jnp
import numpy as np
from jax import lax

NEURONS = 65536
BLOCK = 128
KB = 40
LAYERS = 2
SAMPLES = 256
NBLOCKS = 512
COLS_DEV = 4
CAP = 1


def draw_pattern(key, part):
    devices = NBLOCKS // COLS_DEV
    union_size = devices * CAP
    key_local, key_pick, key_turn = jax.random.split(key, 3)
    local_scores = jax.random.randint(key_local, (LAYERS, devices, devices, COLS_DEV), 0, 1 << 20) * COLS_DEV + jnp.arange(COLS_DEV)
    local_pick = jnp.argsort(local_scores, axis=-1)[..., :CAP]
    union = (jnp.arange(devices)[:, None] * COLS_DEV + local_pick).reshape(LAYERS, devices, union_size)
    pick_scores = jax.random.randint(key_pick, (LAYERS, devices, COLS_DEV, union_size), 0, 1 << 20) * union_size + jnp.arange(union_size)
    picks = jnp.argsort(pick_scores, axis=-1)[..., :KB]
    turn = jax.random.randint(key_turn, (LAYERS, devices), 0, devices) * CAP
    first = (turn[..., None] + jnp.arange(KB)) % union_size
    picks = picks.at[:, :, 0, :].set(first)
    chosen = jnp.take_along_axis(jnp.broadcast_to(union[:, :, None, :], (LAYERS, devices, COLS_DEV, union_size)), picks, axis=-1)
    return chosen.reshape(LAYERS, NBLOCKS, KB).astype(jnp.int32)


def steps_of(rng, extent, cuts, low, top_value):
    factor_of = 1.0
    for dim, shards_of in cuts:
        draws = jax.random.uniform(jax.random.fold_in(jax.random.fold_in(rng, 6), dim), (shards_of,), jnp.float32, low / len(cuts), top_value / len(cuts))
        factor_of = factor_of * jnp.repeat(jnp.exp(draws), extent[dim] // shards_of).reshape((-1,) + (1,) * (len(extent) - 1 - dim))
    return factor_of


def split_up(number_of, total, most, lean):
    loads = [(1 << 20) // math.isqrt(grade ** lean) + 1 for grade in range(2, number_of + 1)]
    surplus, given = total - most - (number_of - 1), [1] * (number_of - 1)
    while surplus > 0:
        candidates = [i for i in range(number_of - 1) if given[i] < most]
        pool, budget = sum([loads[i] for i in candidates]), surplus
        for i in candidates:
            addition = min(most - given[i], max(1, budget * loads[i] // pool), surplus)
            given[i] = given[i] + addition
            surplus = surplus - addition
    return np.array([most] + given)


def ragged(rng, count, total, most, skew):
    if count == 2:
        one = jax.random.randint(rng, (), max(1, total - most), min(most, total - 1) + 1)
        return jnp.stack([one, total - one])
    tallies = jnp.asarray(split_up(count, total, most, skew), jnp.int32)
    pairs = (count - 1) // 2
    giver, taker = tallies[1:1 + 2 * pairs:2], tallies[2:2 + 2 * pairs:2]
    slack = jnp.minimum(giver - 1, most - taker)
    shifted = jax.random.randint(jax.random.fold_in(rng, 1), (pairs,), 0, 1 << 20) % (slack + 1)
    tallies = tallies.at[1:1 + 2 * pairs:2].set(giver - shifted).at[2:2 + 2 * pairs:2].set(taker + shifted)
    return tallies[jax.random.permutation(jax.random.fold_in(rng, 2), count)]


def bell_draw(own_key, dims, scale, limit, pieces=(), dtype=jnp.bfloat16):
    gain = steps_of(own_key, dims, pieces, -0.22, 0.18) if pieces else 1.0
    array = jax.random.normal(own_key, dims, jnp.float32) * scale * gain
    return jnp.minimum(jnp.maximum(array, -limit), limit).astype(dtype)


def setup_inputs(seed: int = 0) -> dict:
    seeds = jax.random.split(jax.random.key(seed), 6)
    return {
        "activations": jnp.clip(16.0 * jax.random.uniform(seeds[0], (SAMPLES, NEURONS), jnp.float32) ** steps_of(seeds[0], (SAMPLES, NEURONS), ((0, 2), (1, 128)), -0.2, 0.2), 0.0, 16.0).astype(jnp.bfloat16),
        "weights": bell_draw(seeds[1], (LAYERS, NBLOCKS, KB, BLOCK, BLOCK), (KB * BLOCK // 4) ** -0.5, 0.15625, ((1, 128), (2, 2))),
        "biases": jnp.clip(-6.0 + 8.0 * jax.random.uniform(seeds[2], (LAYERS, NEURONS), jnp.float32) ** steps_of(seeds[2], (LAYERS, NEURONS), ((1, 128),), -0.2, 0.2), -6.0, 2.0),
        "pattern": draw_pattern(jax.random.fold_in(seeds[5], 71), 0),
        "counts": jax.vmap(lambda own: ragged(own, NBLOCKS, NBLOCKS * KB // 2, KB, 2))(jax.random.split(seeds[4], LAYERS)).reshape((LAYERS, NBLOCKS)).astype(jnp.int32),
    }


def reference(activations, weights, biases, pattern, counts):
    current = activations
    for layer in range(LAYERS):
        blocks = current.reshape(SAMPLES, NBLOCKS, BLOCK)
        live_slots = (jnp.arange(KB)[None, :] < counts[layer][:, None]).astype(jnp.float32)

        def column(packed):
            indices, weight_blocks, live_row = packed
            picked = jnp.take(blocks, indices, axis=1).astype(jnp.float32)
            masked = weight_blocks.astype(jnp.float32) * live_row[:, None, None]
            return jnp.einsum("skb,kbc->sc", picked, masked)

        columns = lax.map(column, (pattern[layer], weights[layer], live_slots))
        total = jnp.transpose(columns, (1, 0, 2)).reshape(SAMPLES, NEURONS)
        current = jnp.clip(total + biases[layer][None, :], 0.0, 32.0).astype(jnp.bfloat16)
    return current
```

```python
import jax
import jax.numpy as jnp
from jax import lax
from jax.experimental import pallas as pl
from jax.experimental.pallas import tpu as pltpu
from jax.sharding import PartitionSpec as P

MESH = pl.DeviceIdType.MESH
NZ = 8
NQ = 4
OWN = 4
BLK = 128
HALF = 64
SLOTS = 40
LAYERS = 2
DEV = 128

A_TX, B_TX, BR_TX, C_TX, CR_TX = range(5)


def wrap(v, n):
    return lax.rem(v + n, n)


def kernel(
    act, w, bias, sel_v, sel_s, inv_s, out,
    gath, pack, recv, far, wts, acc, tab_v, tab_s,
    a_rx, b_rx, br_rx, c_rx, x_rx, tx, w_rx, w_tx, w_in, act_in, tab_rx, tab_tx, tab_in,
):
    me = lax.axis_index("cols")
    core = lax.axis_index("rows")
    sb = 8 + 24 * core
    sc = 32 - 24 * core
    z = lax.rem(me, NZ)
    b = lax.rem(lax.div(me, sb), NQ)
    c = lax.rem(lax.div(me, sc), NQ)

    def zdev(d):
        return me - z + wrap(z + d, NZ)

    def bdev(d):
        return me + (wrap(b + d, NQ) - b) * sb

    def cdev(d):
        return me + (wrap(c + d, NQ) - c) * sc

    def rcopy(src, dst, ssem, rsem, dev):
        return pltpu.make_async_remote_copy(
            src_ref=src, dst_ref=dst, send_sem=ssem, recv_sem=rsem,
            device_id={"cols": dev, "rows": core}, device_id_type=MESH,
        )

    def arrived(ref, sem):
        pltpu.make_async_copy(ref, ref, sem).wait()

    for h in range(2):
        for k in range(OWN):
            pltpu.make_async_copy(
                act.at[pl.ds(h * HALF, HALF), pl.ds(k * BLK, BLK)],
                gath.at[0, b, z, h, k], act_in,
            ).start()
    for l in range(LAYERS):
        pltpu.make_async_copy(
            w.at[l], wts.at[l, :, pl.ds(core * (SLOTS // 2), SLOTS // 2)], w_in.at[l]
        ).start()

    barrier = pltpu.get_barrier_semaphore()
    for dev in (zdev(1), zdev(-1), bdev(1), bdev(-1), cdev(1), cdev(-1), cdev(2)):
        pl.semaphore_signal(
            barrier, inc=1, device_id={"cols": dev, "rows": core}, device_id_type=MESH
        )
    pl.semaphore_signal(
        barrier, inc=1, device_id={"cols": me, "rows": 1 - core}, device_id_type=MESH
    )
    for l in range(LAYERS):
        for j in range(OWN):
            wts[l, j, SLOTS] = jnp.zeros((BLK, BLK), jnp.bfloat16)
    arrived(gath.at[0, b, z], act_in)
    pl.semaphore_wait(barrier, 8)

    table = [
        rcopy(sel_v, tab_v.at[0], tab_tx.at[0], tab_rx.at[0], cdev(-1)),
        rcopy(sel_v, tab_v.at[1], tab_tx.at[1], tab_rx.at[1], cdev(1)),
        rcopy(sel_v, tab_v.at[2], tab_tx.at[2], tab_rx.at[2], cdev(2)),
    ]
    for t in table:
        t.start()

    def wcopy(l):
        part = wts.at[l, :, pl.ds(core * (SLOTS // 2), SLOTS // 2)]
        return pltpu.make_async_remote_copy(
            src_ref=w.at[l], dst_ref=part, send_sem=w_tx.at[l], recv_sem=w_rx.at[l],
            device_id={"cols": me, "rows": 1 - core}, device_id_type=MESH,
        )

    def zidx(i):
        t = lax.div(i + 1, 2)
        return wrap(z + (1 - 2 * lax.rem(i, 2)) * t, NZ)

    def choose(blocks, which):
        picked = blocks[0]
        for k in range(1, OWN):
            picked = jnp.where(which == k, blocks[k], picked)
        return picked

    def send_picks(l, i, off):
        bb = wrap(b + off, NQ)
        zz = zidx(i)
        src = c * sc + bb * sb + zz
        right = tab_s[0, l, src]
        left = tab_s[1, l, src]
        over = tab_s[2, l, src]
        for h in range(2):
            blocks = [gath[l, bb, zz, h, k] for k in range(OWN)]
            pack[l, 0, i, off, h] = choose(blocks, right)
            pack[l, 1, i, off, h] = choose(blocks, left)
            pack[l, h, i, off, 2] = choose(blocks, over)
        for d in range(2):
            rcopy(
                pack.at[l, d, i, off], recv.at[l, d, i, off],
                tx.at[l, C_TX], c_rx.at[l, d, i, off], cdev(1 - 2 * d),
            ).start()

    def relay_picks(l, i, off):
        for d in range(2):
            arrived(recv.at[l, d, i, off], c_rx.at[l, d, i, off])
            rcopy(
                recv.at[l, d, i, off, 2], far.at[l, i, off, d],
                tx.at[l, CR_TX], x_rx.at[l, i], cdev(1 - 2 * d),
            ).start()

    def compute(l, i):
        zz = zidx(i)

        def step(off, carry):
            bb = wrap(b + off, NQ)
            base = bb * sb + zz
            own = sel_s[l * DEV + c * sc + base]
            x = jnp.concatenate(
                [
                    choose(
                        [gath[l, bb, zz, :, k].reshape(BLK, BLK) for k in range(OWN)], own
                    ),
                    recv[l, 0, i, off, pl.ds(0, 2)].reshape(BLK, BLK),
                    recv[l, 1, i, off, pl.ds(0, 2)].reshape(BLK, BLK),
                    far[l, i, off].reshape(BLK, BLK),
                ],
                axis=1,
            )
            rows = []
            for d in (0, -1, 1, 2):
                src = wrap(c + d, NQ) * sc + base
                rows.append(
                    jnp.concatenate(
                        [wts[l, j, inv_s[(l * OWN + j) * DEV + src]] for j in range(OWN)],
                        axis=1,
                    )
                )
            acc[...] += jnp.dot(
                x, jnp.concatenate(rows, axis=0), preferred_element_type=jnp.float32
            )
            return carry

        lax.fori_loop(0, NQ, step, 0)

    def layer(l, carry):
        acc[...] = jnp.zeros_like(acc)

        def turn(i, carry):
            @pl.when(i < NZ)
            def _():
                zz = zidx(i)
                unit = gath.at[l, b, zz]

                @pl.when(i == 0)
                def _():
                    for k, d in ((1, 1), (2, -1)):
                        rcopy(unit, unit, tx.at[l, A_TX], a_rx.at[l, k], zdev(d)).start()

                @pl.when(i >= 1)
                def _():
                    arrived(unit, a_rx.at[l, i])
                    way = 2 * lax.rem(i, 2) - 1

                    @pl.when(i < 5)
                    def _():
                        rcopy(
                            unit, unit, tx.at[l, A_TX], a_rx.at[l, i + 2], zdev(way)
                        ).start()

                    @pl.when((i == 5) | (i == 6))
                    def _():
                        part = gath.at[l, b, zz, i - 5]
                        rcopy(part, part, tx.at[l, A_TX], a_rx.at[l, 7], zdev(way)).start()

                for d in range(2):
                    rcopy(
                        unit, unit, tx.at[l, B_TX], b_rx.at[l, d, i], bdev(1 - 2 * d)
                    ).start()

                @pl.when((l == 0) & (i == 0))
                def _():
                    wcopy(0).start()
                    wcopy(1).start()
                    for t in table:
                        t.wait()
                    tab = pltpu.make_async_copy(tab_v, tab_s, tab_in)
                    tab.start()
                    tab.wait()

                send_picks(l, i, 0)

            @pl.when((i >= 1) & (i < NZ + 1))
            def _():
                j = i - 1
                zz = zidx(j)
                for d in range(2):
                    bb = wrap(b - 1 + 2 * d, NQ)
                    arrived(gath.at[l, bb, zz], b_rx.at[l, d, j])
                    part = gath.at[l, bb, zz, d]
                    rcopy(
                        part, part, tx.at[l, BR_TX], br_rx.at[l, j], bdev(1 - 2 * d)
                    ).start()
                send_picks(l, j, 1)
                send_picks(l, j, 3)

            @pl.when((i >= 2) & (i < NZ + 2))
            def _():
                j = i - 2
                arrived(gath.at[l, wrap(b + 2, NQ), zidx(j)], br_rx.at[l, j])
                send_picks(l, j, 2)

            @pl.when((i >= 1) & (i < NZ + 1))
            def _():
                relay_picks(l, i - 1, 0)

            @pl.when((i >= 2) & (i < NZ + 2))
            def _():
                relay_picks(l, i - 2, 1)
                relay_picks(l, i - 2, 3)

            @pl.when((i >= 3) & (i < NZ + 3))
            def _():
                relay_picks(l, i - 3, 2)

            @pl.when(i >= 4)
            def _():
                j = i - 4

                @pl.when((l == 0) & (j == 0))
                def _():
                    for k in range(LAYERS):
                        wcopy(k).wait_recv()
                        arrived(
                            wts.at[k, :, pl.ds(core * (SLOTS // 2), SLOTS // 2)],
                            w_in.at[k],
                        )

                arrived(far.at[l, j], x_rx.at[l, j])
                compute(l, j)

            return carry

        lax.fori_loop(0, NZ + 4, turn, 0)
        total = acc[...] + bias[pl.ds(l, 1), :]
        result = jnp.minimum(jnp.maximum(total, 0.0), 32.0).astype(jnp.bfloat16)

        @pl.when(l + 1 < LAYERS)
        def _():
            for h in range(2):
                for k in range(OWN):
                    gath[1, b, z, h, k] = result[
                        h * HALF : (h + 1) * HALF, k * BLK : (k + 1) * BLK
                    ]

        @pl.when(l + 1 == LAYERS)
        def _():
            out[...] = result

        return carry

    lax.fori_loop(0, LAYERS, layer, 0)
    for l in range(LAYERS):
        arrived(gath.at[l, 0, pl.ds(0, 7)], tx.at[l, A_TX])
        arrived(gath.at[l, pl.ds(0, 2)], tx.at[l, B_TX])
        arrived(gath.at[l, 0], tx.at[l, BR_TX])
        arrived(pack.at[l], tx.at[l, C_TX])
        arrived(far.at[l], tx.at[l, CR_TX])
        wcopy(l).wait_send()


def tables(pattern, counts):
    source = pattern // OWN
    chips = jnp.arange(DEV, dtype=jnp.int32)
    hit = source[..., None] == chips
    pick = jnp.max(jnp.where(hit, (pattern % OWN)[..., None], 0), axis=(1, 2))
    slot = jnp.arange(SLOTS, dtype=jnp.int32)[None, None, :, None]
    live = hit & (slot < counts[:, :, None, None])
    inverse = jnp.min(jnp.where(live, slot, SLOTS), axis=2)
    return pick, inverse


def per_device(activations, weights, biases, pattern, counts):
    pick, inverse = tables(pattern, counts)
    pick_v = jnp.pad(pick, ((0, 8 - LAYERS), (0, 0)))
    bf16, sem = jnp.bfloat16, pltpu.SemaphoreType.DMA
    vmem = pl.BlockSpec(memory_space=pltpu.VMEM)
    smem = pl.BlockSpec(memory_space=pltpu.SMEM)
    hbm = pl.BlockSpec(memory_space=pl.ANY)
    return pl.pallas_call(
        kernel,
        out_shape=jax.ShapeDtypeStruct(activations.shape, bf16),
        in_specs=[hbm, hbm, vmem, vmem, smem, smem],
        out_specs=vmem,
        scratch_shapes=[
            pltpu.VMEM((LAYERS, NQ, NZ, 2, OWN, HALF, BLK), bf16),
            pltpu.VMEM((LAYERS, 2, NZ, NQ, 3, HALF, BLK), bf16),
            pltpu.VMEM((LAYERS, 2, NZ, NQ, 3, HALF, BLK), bf16),
            pltpu.VMEM((LAYERS, NZ, NQ, 2, HALF, BLK), bf16),
            pltpu.VMEM((LAYERS, OWN, SLOTS + 1, BLK, BLK), bf16),
            pltpu.VMEM((2 * HALF, OWN * BLK), jnp.float32),
            pltpu.VMEM((3, 8, DEV), jnp.int32),
            pltpu.SMEM((3, 8, DEV), jnp.int32),
            sem((LAYERS, NZ)),
            sem((LAYERS, 2, NZ)),
            sem((LAYERS, NZ)),
            sem((LAYERS, 2, NZ, NQ)),
            sem((LAYERS, NZ)),
            sem((LAYERS, 5)),
            sem((LAYERS,)),
            sem((LAYERS,)),
            sem((LAYERS,)),
            sem,
            sem((3,)),
            sem((3,)),
            sem,
        ],
        compiler_params=pltpu.CompilerParams(
            collective_id=0, has_side_effects=True, vmem_limit_bytes=60 << 20
        ),
    )(activations, weights, biases, pick_v, pick.reshape(-1), inverse.reshape(-1))


def solution(mesh):
    return jax.shard_map(
        per_device,
        mesh=mesh,
        in_specs=(
            P("rows", "cols"),
            P(None, "cols", "rows", None, None),
            P(None, "cols"),
            P(None, "cols", None),
            P(None, "cols"),
        ),
        out_specs=P("rows", "cols"),
        check_vma=False,
    )
```

```python
import jax
import jax.numpy as jnp
from jax import lax
from jax.experimental import pallas as pl
from jax.experimental.pallas import tpu as pltpu
from jax.sharding import PartitionSpec as P

MESH = pl.DeviceIdType.MESH
NZ = 8
NQ = 4
OWN = 4
BLK = 128
HALF = 64
SLOTS = 40
LAYERS = 2
DEV = 128

A_TX, B_TX, BR_TX, C_TX, CR_TX, E_TX = range(6)


def wrap(v, n):
    return lax.rem(v + n, n)


def kernel(
    act, w, bias, sel_v, sel_s, inv_s, out,
    gath, pack, recv, far, wts, acc, tab_v, tab_s,
    a_rx, b_rx, br_rx, e_rx, c_rx, x_rx, tx, w_rx, w_tx, w_in, act_in, tab_rx, tab_tx, tab_in,
):
    me = lax.axis_index("cols")
    core = lax.axis_index("rows")
    sb = 8 + 24 * core
    sc = 32 - 24 * core
    z = lax.rem(me, NZ)
    b = lax.rem(lax.div(me, sb), NQ)
    c = lax.rem(lax.div(me, sc), NQ)

    def zdev(d):
        return me - z + wrap(z + d, NZ)

    def bdev(d):
        return me + (wrap(b + d, NQ) - b) * sb

    def cdev(d):
        return me + (wrap(c + d, NQ) - c) * sc

    def rcopy(src, dst, ssem, rsem, dev):
        return pltpu.make_async_remote_copy(
            src_ref=src, dst_ref=dst, send_sem=ssem, recv_sem=rsem,
            device_id={"cols": dev, "rows": core}, device_id_type=MESH,
        )

    def arrived(ref, sem):
        pltpu.make_async_copy(ref, ref, sem).wait()

    for h in range(2):
        for k in range(OWN):
            pltpu.make_async_copy(
                act.at[pl.ds(h * HALF, HALF), pl.ds(k * BLK, BLK)],
                gath.at[0, b, z, h, k], act_in,
            ).start()
    for l in range(LAYERS):
        pltpu.make_async_copy(
            w.at[l], wts.at[l, :, pl.ds(core * (SLOTS // 2), SLOTS // 2)], w_in.at[l]
        ).start()

    barrier = pltpu.get_barrier_semaphore()
    for dev in (zdev(1), zdev(-1), bdev(1), bdev(-1), cdev(1), cdev(-1), cdev(2)):
        pl.semaphore_signal(
            barrier, inc=1, device_id={"cols": dev, "rows": core}, device_id_type=MESH
        )
    pl.semaphore_signal(
        barrier, inc=1, device_id={"cols": me, "rows": 1 - core}, device_id_type=MESH
    )
    for l in range(LAYERS):
        for j in range(OWN):
            wts[l, j, SLOTS] = jnp.zeros((BLK, BLK), jnp.bfloat16)
    arrived(gath.at[0, b, z], act_in)
    pl.semaphore_wait(barrier, 8)

    table = [
        rcopy(sel_v, tab_v.at[0], tab_tx.at[0], tab_rx.at[0], cdev(-1)),
        rcopy(sel_v, tab_v.at[1], tab_tx.at[1], tab_rx.at[1], cdev(1)),
        rcopy(sel_v, tab_v.at[2], tab_tx.at[2], tab_rx.at[2], cdev(2)),
    ]
    for t in table:
        t.start()

    def wcopy(l):
        part = wts.at[l, :, pl.ds(core * (SLOTS // 2), SLOTS // 2)]
        return pltpu.make_async_remote_copy(
            src_ref=w.at[l], dst_ref=part, send_sem=w_tx.at[l], recv_sem=w_rx.at[l],
            device_id={"cols": me, "rows": 1 - core}, device_id_type=MESH,
        )

    def zidx(i):
        t = lax.div(i + 1, 2)
        return wrap(z + (1 - 2 * lax.rem(i, 2)) * t, NZ)

    def choose(blocks, which):
        picked = blocks[0]
        for k in range(1, OWN):
            picked = jnp.where(which == k, blocks[k], picked)
        return picked

    def relay_other(l, i, off):
        bb = wrap(b + off, NQ)
        unit = gath.at[l, bb, zidx(i), 1]

        @pl.when(i == 0)
        def _():
            for k, d in ((1, 1), (2, -1)):
                rcopy(unit, unit, tx.at[l, E_TX], e_rx.at[l, off - 1, k], zdev(d)).start()

        @pl.when(i >= 1)
        def _():
            arrived(unit, e_rx.at[l, off - 1, i])
            way = 2 * lax.rem(i, 2) - 1

            @pl.when(i < 5)
            def _():
                rcopy(
                    unit, unit, tx.at[l, E_TX], e_rx.at[l, off - 1, i + 2], zdev(way)
                ).start()

            @pl.when((i == 5) | (i == 6))
            def _():
                part = gath.at[l, bb, zidx(i), 1, pl.ds(2 * (i - 5), 2)]
                rcopy(
                    part, part, tx.at[l, E_TX], e_rx.at[l, off - 1, 7], zdev(way)
                ).start()

    def send_picks(l, i, off):
        bb = wrap(b + off, NQ)
        zz = zidx(i)
        src = c * sc + bb * sb + zz
        right = tab_s[0, l, src]
        left = tab_s[1, l, src]
        over = tab_s[2, l, src]
        for h in range(2):
            blocks = [gath[l, bb, zz, h, k] for k in range(OWN)]
            pack[l, 0, i, off, h] = choose(blocks, right)
            pack[l, 1, i, off, h] = choose(blocks, left)
            pack[l, h, i, off, 2] = choose(blocks, over)
        for d in range(2):
            rcopy(
                pack.at[l, d, i, off], recv.at[l, d, i, off],
                tx.at[l, C_TX], c_rx.at[l, d, i, off], cdev(1 - 2 * d),
            ).start()

    def relay_picks(l, i, off):
        for d in range(2):
            arrived(recv.at[l, d, i, off], c_rx.at[l, d, i, off])
            rcopy(
                recv.at[l, d, i, off, 2], far.at[l, i, off, d],
                tx.at[l, CR_TX], x_rx.at[l, i], cdev(1 - 2 * d),
            ).start()

    def compute(l, i):
        zz = zidx(i)

        def step(off, carry):
            bb = wrap(b + off, NQ)
            base = bb * sb + zz
            own = sel_s[l * DEV + c * sc + base]
            x = jnp.concatenate(
                [
                    choose(
                        [gath[l, bb, zz, :, k].reshape(BLK, BLK) for k in range(OWN)], own
                    ),
                    recv[l, 0, i, off, pl.ds(0, 2)].reshape(BLK, BLK),
                    recv[l, 1, i, off, pl.ds(0, 2)].reshape(BLK, BLK),
                    far[l, i, off].reshape(BLK, BLK),
                ],
                axis=1,
            )
            rows = []
            for d in (0, -1, 1, 2):
                src = wrap(c + d, NQ) * sc + base
                rows.append(
                    jnp.concatenate(
                        [wts[l, j, inv_s[(l * OWN + j) * DEV + src]] for j in range(OWN)],
                        axis=1,
                    )
                )
            acc[...] += jnp.dot(
                x, jnp.concatenate(rows, axis=0), preferred_element_type=jnp.float32
            )
            return carry

        lax.fori_loop(0, NQ, step, 0)

    def layer(l, carry):
        acc[...] = jnp.zeros_like(acc)

        def turn(i, carry):
            @pl.when(i < NZ)
            def _():
                zz = zidx(i)
                unit = gath.at[l, b, zz]

                @pl.when(i == 0)
                def _():
                    for k, d in ((1, 1), (2, -1)):
                        rcopy(unit, unit, tx.at[l, A_TX], a_rx.at[l, k], zdev(d)).start()

                @pl.when(i >= 1)
                def _():
                    arrived(unit, a_rx.at[l, i])
                    way = 2 * lax.rem(i, 2) - 1

                    @pl.when(i < 5)
                    def _():
                        rcopy(
                            unit, unit, tx.at[l, A_TX], a_rx.at[l, i + 2], zdev(way)
                        ).start()

                    @pl.when((i == 5) | (i == 6))
                    def _():
                        part = gath.at[l, b, zz, i - 5]
                        rcopy(part, part, tx.at[l, A_TX], a_rx.at[l, 7], zdev(way)).start()

                for d in range(2):
                    @pl.when(i == 0)
                    def _():
                        rcopy(
                            unit, unit, tx.at[l, B_TX], b_rx.at[l, d, i], bdev(1 - 2 * d)
                        ).start()

                    @pl.when(i >= 1)
                    def _():
                        part = gath.at[l, b, zz, 0]
                        rcopy(
                            part, part, tx.at[l, B_TX], b_rx.at[l, d, i], bdev(1 - 2 * d)
                        ).start()

                @pl.when((l == 0) & (i == 0))
                def _():
                    wcopy(0).start()
                    wcopy(1).start()
                    for t in table:
                        t.wait()
                    tab = pltpu.make_async_copy(tab_v, tab_s, tab_in)
                    tab.start()
                    tab.wait()

                send_picks(l, i, 0)

            @pl.when((i >= 1) & (i < NZ + 1))
            def _():
                j = i - 1
                zz = zidx(j)
                for d in range(2):
                    bb = wrap(b - 1 + 2 * d, NQ)

                    @pl.when(j == 0)
                    def _():
                        arrived(gath.at[l, bb, zz], b_rx.at[l, d, j])
                        part = gath.at[l, bb, zz, d]
                        rcopy(
                            part, part, tx.at[l, BR_TX], br_rx.at[l, j], bdev(1 - 2 * d)
                        ).start()

                    @pl.when(j >= 1)
                    def _():
                        arrived(gath.at[l, bb, zz, 0], b_rx.at[l, d, j])
                        part = gath.at[l, bb, zz, 0, pl.ds(2 * d, 2)]
                        rcopy(
                            part, part, tx.at[l, BR_TX], br_rx.at[l, j], bdev(1 - 2 * d)
                        ).start()
                relay_other(l, j, 1)
                relay_other(l, j, 3)
                send_picks(l, j, 1)
                send_picks(l, j, 3)

            @pl.when((i >= 2) & (i < NZ + 2))
            def _():
                j = i - 2

                @pl.when(j == 0)
                def _():
                    arrived(gath.at[l, wrap(b + 2, NQ), zidx(j)], br_rx.at[l, j])

                @pl.when(j >= 1)
                def _():
                    arrived(gath.at[l, wrap(b + 2, NQ), zidx(j), 0], br_rx.at[l, j])

                relay_other(l, j, 2)
                send_picks(l, j, 2)

            @pl.when((i >= 1) & (i < NZ + 1))
            def _():
                relay_picks(l, i - 1, 0)

            @pl.when((i >= 2) & (i < NZ + 2))
            def _():
                relay_picks(l, i - 2, 1)
                relay_picks(l, i - 2, 3)

            @pl.when((i >= 3) & (i < NZ + 3))
            def _():
                relay_picks(l, i - 3, 2)

            @pl.when(i >= 4)
            def _():
                j = i - 4

                @pl.when((l == 0) & (j == 0))
                def _():
                    for k in range(LAYERS):
                        wcopy(k).wait_recv()
                        arrived(
                            wts.at[k, :, pl.ds(core * (SLOTS // 2), SLOTS // 2)],
                            w_in.at[k],
                        )

                arrived(far.at[l, j], x_rx.at[l, j])
                compute(l, j)

            return carry

        lax.fori_loop(0, NZ + 4, turn, 0)
        total = acc[...] + bias[pl.ds(l, 1), :]
        result = jnp.minimum(jnp.maximum(total, 0.0), 32.0).astype(jnp.bfloat16)

        @pl.when(l + 1 < LAYERS)
        def _():
            for h in range(2):
                for k in range(OWN):
                    gath[1, b, z, h, k] = result[
                        h * HALF : (h + 1) * HALF, k * BLK : (k + 1) * BLK
                    ]

        @pl.when(l + 1 == LAYERS)
        def _():
            out[...] = result

        return carry

    lax.fori_loop(0, LAYERS, layer, 0)
    for l in range(LAYERS):
        arrived(gath.at[l, 0, pl.ds(0, 7)], tx.at[l, A_TX])
        arrived(gath.at[l, pl.ds(0, 3), pl.ds(0, 3)], tx.at[l, B_TX])
        arrived(gath.at[l, pl.ds(0, 3), pl.ds(0, 3), 0], tx.at[l, BR_TX])
        arrived(gath.at[l, pl.ds(0, 3), pl.ds(0, 7), 0], tx.at[l, E_TX])
        arrived(pack.at[l], tx.at[l, C_TX])
        arrived(far.at[l], tx.at[l, CR_TX])
        wcopy(l).wait_send()


def tables(pattern, counts):
    source = pattern // OWN
    chips = jnp.arange(DEV, dtype=jnp.int32)
    hit = source[..., None] == chips
    pick = jnp.max(jnp.where(hit, (pattern % OWN)[..., None], 0), axis=(1, 2))
    slot = jnp.arange(SLOTS, dtype=jnp.int32)[None, None, :, None]
    live = hit & (slot < counts[:, :, None, None])
    inverse = jnp.min(jnp.where(live, slot, SLOTS), axis=2)
    return pick, inverse


def per_device(activations, weights, biases, pattern, counts):
    pick, inverse = tables(pattern, counts)
    pick_v = jnp.pad(pick, ((0, 8 - LAYERS), (0, 0)))
    bf16, sem = jnp.bfloat16, pltpu.SemaphoreType.DMA
    vmem = pl.BlockSpec(memory_space=pltpu.VMEM)
    smem = pl.BlockSpec(memory_space=pltpu.SMEM)
    hbm = pl.BlockSpec(memory_space=pl.ANY)
    return pl.pallas_call(
        kernel,
        out_shape=jax.ShapeDtypeStruct(activations.shape, bf16),
        in_specs=[hbm, hbm, vmem, vmem, smem, smem],
        out_specs=vmem,
        scratch_shapes=[
            pltpu.VMEM((LAYERS, NQ, NZ, 2, OWN, HALF, BLK), bf16),
            pltpu.VMEM((LAYERS, 2, NZ, NQ, 3, HALF, BLK), bf16),
            pltpu.VMEM((LAYERS, 2, NZ, NQ, 3, HALF, BLK), bf16),
            pltpu.VMEM((LAYERS, NZ, NQ, 2, HALF, BLK), bf16),
            pltpu.VMEM((LAYERS, OWN, SLOTS + 1, BLK, BLK), bf16),
            pltpu.VMEM((2 * HALF, OWN * BLK), jnp.float32),
            pltpu.VMEM((3, 8, DEV), jnp.int32),
            pltpu.SMEM((3, 8, DEV), jnp.int32),
            sem((LAYERS, NZ)),
            sem((LAYERS, 2, NZ)),
            sem((LAYERS, NZ)),
            sem((LAYERS, NQ - 1, NZ)),
            sem((LAYERS, 2, NZ, NQ)),
            sem((LAYERS, NZ)),
            sem((LAYERS, 6)),
            sem((LAYERS,)),
            sem((LAYERS,)),
            sem((LAYERS,)),
            sem,
            sem((3,)),
            sem((3,)),
            sem,
        ],
        compiler_params=pltpu.CompilerParams(
            collective_id=0, has_side_effects=True, vmem_limit_bytes=60 << 20
        ),
    )(activations, weights, biases, pick_v, pick.reshape(-1), inverse.reshape(-1))


def solution(mesh):
    return jax.shard_map(
        per_device,
        mesh=mesh,
        in_specs=(
            P("rows", "cols"),
            P(None, "cols", "rows", None, None),
            P(None, "cols"),
            P(None, "cols", None),
            P(None, "cols"),
        ),
        out_specs=P("rows", "cols"),
        check_vma=False,
    )
```

```python
import jax
import jax.numpy as jnp
from jax import lax
from jax.experimental import pallas as pl
from jax.experimental.pallas import tpu as pltpu
from jax.sharding import PartitionSpec as P

MESH = pl.DeviceIdType.MESH
NZ = 8
NQ = 4
OWN = 4
BLK = 128
HALF = 64
SLOTS = 40
LAYERS = 2
DEV = 128

A_TX, B_TX, BR_TX, C_TX, CR_TX, E_TX = range(6)


def wrap(v, n):
    return lax.rem(v + n, n)


def kernel(
    act, w, bias, sel_v, sel_s, inv_s, out,
    gath, pack, recv, far, wts, acc, tab_v, tab_s,
    a_rx, b_rx, br_rx, e_rx, c_rx, x_rx, tx, w_rx, w_tx, w_in, act_in, tab_rx, tab_tx, tab_in,
):
    me = lax.axis_index("cols")
    core = lax.axis_index("rows")
    sb = 8 + 24 * core
    sc = 32 - 24 * core
    z = lax.rem(me, NZ)
    b = lax.rem(lax.div(me, sb), NQ)
    c = lax.rem(lax.div(me, sc), NQ)

    def zdev(d):
        return me - z + wrap(z + d, NZ)

    def bdev(d):
        return me + (wrap(b + d, NQ) - b) * sb

    def cdev(d):
        return me + (wrap(c + d, NQ) - c) * sc

    def rcopy(src, dst, ssem, rsem, dev):
        return pltpu.make_async_remote_copy(
            src_ref=src, dst_ref=dst, send_sem=ssem, recv_sem=rsem,
            device_id={"cols": dev, "rows": core}, device_id_type=MESH,
        )

    def arrived(ref, sem):
        pltpu.make_async_copy(ref, ref, sem).wait()

    for h in range(2):
        for k in range(OWN):
            pltpu.make_async_copy(
                act.at[pl.ds(h * HALF, HALF), pl.ds(k * BLK, BLK)],
                gath.at[0, b, z, h, k], act_in,
            ).start()
    for l in range(LAYERS):
        pltpu.make_async_copy(
            w.at[l], wts.at[l, :, pl.ds(core * (SLOTS // 2), SLOTS // 2)], w_in.at[l]
        ).start()

    barrier = pltpu.get_barrier_semaphore()
    for dev in (zdev(1), zdev(-1), bdev(1), bdev(-1), cdev(1), cdev(-1), cdev(2)):
        pl.semaphore_signal(
            barrier, inc=1, device_id={"cols": dev, "rows": core}, device_id_type=MESH
        )
    pl.semaphore_signal(
        barrier, inc=1, device_id={"cols": me, "rows": 1 - core}, device_id_type=MESH
    )
    for l in range(LAYERS):
        for j in range(OWN):
            wts[l, j, SLOTS] = jnp.zeros((BLK, BLK), jnp.bfloat16)
    arrived(gath.at[0, b, z], act_in)
    pl.semaphore_wait(barrier, 8)

    table = [
        rcopy(sel_v, tab_v.at[0], tab_tx.at[0], tab_rx.at[0], cdev(-1)),
        rcopy(sel_v, tab_v.at[1], tab_tx.at[1], tab_rx.at[1], cdev(1)),
        rcopy(sel_v, tab_v.at[2], tab_tx.at[2], tab_rx.at[2], cdev(2)),
    ]
    for t in table:
        t.start()

    def wcopy(l):
        part = wts.at[l, :, pl.ds(core * (SLOTS // 2), SLOTS // 2)]
        return pltpu.make_async_remote_copy(
            src_ref=w.at[l], dst_ref=part, send_sem=w_tx.at[l], recv_sem=w_rx.at[l],
            device_id={"cols": me, "rows": 1 - core}, device_id_type=MESH,
        )

    def zidx(i):
        t = lax.div(i + 1, 2)
        return wrap(z + (1 - 2 * lax.rem(i, 2)) * t, NZ)

    def choose(blocks, which):
        picked = blocks[0]
        for k in range(1, OWN):
            picked = jnp.where(which == k, blocks[k], picked)
        return picked

    def relay_other(l, i, off):
        bb = wrap(b + off, NQ)
        unit = gath.at[l, bb, zidx(i), 1]

        @pl.when(i == 0)
        def _():
            for k, d in ((1, 1), (2, -1)):
                rcopy(unit, unit, tx.at[l, E_TX], e_rx.at[l, off - 1, k], zdev(d)).start()

        @pl.when(i >= 1)
        def _():
            arrived(unit, e_rx.at[l, off - 1, i])
            way = 2 * lax.rem(i, 2) - 1

            @pl.when(i < 5)
            def _():
                rcopy(
                    unit, unit, tx.at[l, E_TX], e_rx.at[l, off - 1, i + 2], zdev(way)
                ).start()

            @pl.when((i == 5) | (i == 6))
            def _():
                part = gath.at[l, bb, zidx(i), 1, pl.ds(2 * (i - 5), 2)]
                rcopy(
                    part, part, tx.at[l, E_TX], e_rx.at[l, off - 1, 7], zdev(way)
                ).start()

    def send_picks(l, i, off):
        bb = wrap(b + off, NQ)
        zz = zidx(i)
        src = c * sc + bb * sb + zz
        right = tab_s[0, l, src]
        left = tab_s[1, l, src]
        over = tab_s[2, l, src]
        for h in range(2):
            blocks = [gath[l, bb, zz, h, k] for k in range(OWN)]
            pack[l, 0, i, off, h] = choose(blocks, right)
            pack[l, 1, i, off, h] = choose(blocks, left)
            pack[l, h, i, off, 2] = choose(blocks, over)
        for d in range(2):
            rcopy(
                pack.at[l, d, i, off], recv.at[l, d, i, off],
                tx.at[l, C_TX], c_rx.at[l, d, i, off], cdev(1 - 2 * d),
            ).start()

    def relay_picks(l, i, off):
        for d in range(2):
            arrived(recv.at[l, d, i, off], c_rx.at[l, d, i, off])
            rcopy(
                recv.at[l, d, i, off, 2], far.at[l, i, off, d],
                tx.at[l, CR_TX], x_rx.at[l, i], cdev(1 - 2 * d),
            ).start()

    def compute(l, i):
        zz = zidx(i)

        def step(off, carry):
            bb = wrap(b + off, NQ)
            base = bb * sb + zz
            own = sel_s[l * DEV + c * sc + base]
            x = jnp.concatenate(
                [
                    choose(
                        [gath[l, bb, zz, :, k].reshape(BLK, BLK) for k in range(OWN)], own
                    ),
                    recv[l, 0, i, off, pl.ds(0, 2)].reshape(BLK, BLK),
                    recv[l, 1, i, off, pl.ds(0, 2)].reshape(BLK, BLK),
                    far[l, i, off].reshape(BLK, BLK),
                ],
                axis=1,
            )
            rows = []
            for d in (0, -1, 1, 2):
                src = wrap(c + d, NQ) * sc + base
                rows.append(
                    jnp.concatenate(
                        [wts[l, j, inv_s[(l * OWN + j) * DEV + src]] for j in range(OWN)],
                        axis=1,
                    )
                )
            acc[...] += jnp.dot(
                x, jnp.concatenate(rows, axis=0), preferred_element_type=jnp.float32
            )
            return carry

        lax.fori_loop(0, NQ, step, 0)

    def layer(l, carry):
        acc[...] = jnp.zeros_like(acc)

        def turn(i, carry):
            @pl.when(i < NZ)
            def _():
                zz = zidx(i)
                unit = gath.at[l, b, zz]

                @pl.when(i == 0)
                def _():
                    for k, d in ((1, 1), (2, -1)):
                        rcopy(unit, unit, tx.at[l, A_TX], a_rx.at[l, k], zdev(d)).start()

                @pl.when(i >= 1)
                def _():
                    arrived(unit, a_rx.at[l, i])
                    way = 2 * lax.rem(i, 2) - 1

                    @pl.when(i < 5)
                    def _():
                        rcopy(
                            unit, unit, tx.at[l, A_TX], a_rx.at[l, i + 2], zdev(way)
                        ).start()

                    @pl.when((i == 5) | (i == 6))
                    def _():
                        part = gath.at[l, b, zz, i - 5]
                        rcopy(part, part, tx.at[l, A_TX], a_rx.at[l, 7], zdev(way)).start()

                for d in range(2):
                    @pl.when(i == 0)
                    def _():
                        rcopy(
                            unit, unit, tx.at[l, B_TX], b_rx.at[l, d, i], bdev(1 - 2 * d)
                        ).start()

                    @pl.when(i >= 1)
                    def _():
                        part = gath.at[l, b, zz, 0]
                        rcopy(
                            part, part, tx.at[l, B_TX], b_rx.at[l, d, i], bdev(1 - 2 * d)
                        ).start()

                @pl.when((l == 0) & (i == 0))
                def _():
                    wcopy(0).start()
                    wcopy(1).start()
                    for t in table:
                        t.wait()
                    tab = pltpu.make_async_copy(tab_v, tab_s, tab_in)
                    tab.start()
                    tab.wait()

                send_picks(l, i, 0)

            @pl.when((i >= 1) & (i < NZ + 1))
            def _():
                j = i - 1
                zz = zidx(j)
                for d in range(2):
                    bb = wrap(b - 1 + 2 * d, NQ)

                    @pl.when(j == 0)
                    def _():
                        arrived(gath.at[l, bb, zz], b_rx.at[l, d, j])
                        part = gath.at[l, bb, zz, d]
                        rcopy(
                            part, part, tx.at[l, BR_TX], br_rx.at[l, j], bdev(1 - 2 * d)
                        ).start()

                    @pl.when(j >= 1)
                    def _():
                        arrived(gath.at[l, bb, zz, 0], b_rx.at[l, d, j])
                        part = gath.at[l, bb, zz, 0, pl.ds(2 * d, 2)]
                        rcopy(
                            part, part, tx.at[l, BR_TX], br_rx.at[l, j], bdev(1 - 2 * d)
                        ).start()
                relay_other(l, j, 1)
                relay_other(l, j, 3)
                send_picks(l, j, 1)
                send_picks(l, j, 3)

            @pl.when((i >= 2) & (i < NZ + 2))
            def _():
                j = i - 2

                @pl.when(j == 0)
                def _():
                    arrived(gath.at[l, wrap(b + 2, NQ), zidx(j)], br_rx.at[l, j])

                @pl.when(j >= 1)
                def _():
                    arrived(gath.at[l, wrap(b + 2, NQ), zidx(j), 0], br_rx.at[l, j])

                relay_other(l, j, 2)
                send_picks(l, j, 2)

            @pl.when((i >= 1) & (i < NZ + 1))
            def _():
                relay_picks(l, i - 1, 0)

            @pl.when((i >= 2) & (i < NZ + 2))
            def _():
                relay_picks(l, i - 2, 1)
                relay_picks(l, i - 2, 3)

            @pl.when((i >= 3) & (i < NZ + 3))
            def _():
                relay_picks(l, i - 3, 2)

            @pl.when(i >= 4)
            def _():
                j = i - 4

                @pl.when((l == 0) & (j == 0))
                def _():
                    for k in range(LAYERS):
                        wcopy(k).wait_recv()
                        arrived(
                            wts.at[k, :, pl.ds(core * (SLOTS // 2), SLOTS // 2)],
                            w_in.at[k],
                        )

                arrived(far.at[l, j], x_rx.at[l, j])
                compute(l, j)

            return carry

        lax.fori_loop(0, NZ + 4, turn, 0)
        total = acc[...] + bias[pl.ds(l, 1), :]
        result = jnp.minimum(jnp.maximum(total, 0.0), 32.0).astype(jnp.bfloat16)

        @pl.when(l + 1 < LAYERS)
        def _():
            for h in range(2):
                for k in range(OWN):
                    gath[1, b, z, h, k] = result[
                        h * HALF : (h + 1) * HALF, k * BLK : (k + 1) * BLK
                    ]

        @pl.when(l + 1 == LAYERS)
        def _():
            out[...] = result

        return carry

    lax.fori_loop(0, LAYERS, layer, 0)
    for l in range(LAYERS):
        arrived(gath.at[l, 0, pl.ds(0, 7)], tx.at[l, A_TX])
        arrived(gath.at[l, pl.ds(0, 3), pl.ds(0, 3)], tx.at[l, B_TX])
        arrived(gath.at[l, pl.ds(0, 3), pl.ds(0, 3), 0], tx.at[l, BR_TX])
        arrived(gath.at[l, pl.ds(0, 3), pl.ds(0, 7), 0], tx.at[l, E_TX])
        arrived(pack.at[l], tx.at[l, C_TX])
        arrived(far.at[l], tx.at[l, CR_TX])
        wcopy(l).wait_send()


def tables(pattern, counts):
    source = pattern >> 2
    chips = jnp.arange(DEV, dtype=jnp.int32)
    hit = source[..., None] == chips
    pick = jnp.max(jnp.where(hit, (pattern & (OWN - 1))[..., None], 0), axis=(1, 2))
    slot = jnp.arange(SLOTS, dtype=jnp.int32)[None, None, :, None]
    live = hit & (slot < counts[:, :, None, None])
    inverse = jnp.min(jnp.where(live, slot, SLOTS), axis=2)
    return pick, inverse


def per_device(activations, weights, biases, pattern, counts):
    pick, inverse = tables(pattern, counts)
    bf16, sem = jnp.bfloat16, pltpu.SemaphoreType.DMA
    vmem = pl.BlockSpec(memory_space=pltpu.VMEM)
    smem = pl.BlockSpec(memory_space=pltpu.SMEM)
    hbm = pl.BlockSpec(memory_space=pl.ANY)
    return pl.pallas_call(
        kernel,
        out_shape=jax.ShapeDtypeStruct(activations.shape, bf16),
        in_specs=[hbm, hbm, vmem, vmem, smem, smem],
        out_specs=vmem,
        scratch_shapes=[
            pltpu.VMEM((LAYERS, NQ, NZ, 2, OWN, HALF, BLK), bf16),
            pltpu.VMEM((LAYERS, 2, NZ, NQ, 3, HALF, BLK), bf16),
            pltpu.VMEM((LAYERS, 2, NZ, NQ, 3, HALF, BLK), bf16),
            pltpu.VMEM((LAYERS, NZ, NQ, 2, HALF, BLK), bf16),
            pltpu.VMEM((LAYERS, OWN, SLOTS + 1, BLK, BLK), bf16),
            pltpu.VMEM((2 * HALF, OWN * BLK), jnp.float32),
            pltpu.VMEM((3, LAYERS, DEV), jnp.int32),
            pltpu.SMEM((3, LAYERS, DEV), jnp.int32),
            sem((LAYERS, NZ)),
            sem((LAYERS, 2, NZ)),
            sem((LAYERS, NZ)),
            sem((LAYERS, NQ - 1, NZ)),
            sem((LAYERS, 2, NZ, NQ)),
            sem((LAYERS, NZ)),
            sem((LAYERS, 6)),
            sem((LAYERS,)),
            sem((LAYERS,)),
            sem((LAYERS,)),
            sem,
            sem((3,)),
            sem((3,)),
            sem,
        ],
        compiler_params=pltpu.CompilerParams(
            collective_id=0, has_side_effects=True, vmem_limit_bytes=60 << 20
        ),
    )(activations, weights, biases, pick, pick.reshape(-1), inverse.reshape(-1))


def solution(mesh):
    return jax.shard_map(
        per_device,
        mesh=mesh,
        in_specs=(
            P("rows", "cols"),
            P(None, "cols", "rows", None, None),
            P(None, "cols"),
            P(None, "cols", None),
            P(None, "cols"),
        ),
        out_specs=P("rows", "cols"),
        check_vma=False,
    )
```
